256 devices in a mesh: ctx: 32 (over x, z), head: 8 (over y, core).
Axes of the slice: x: 4, y: 4, z: 8, core: 2. Of those that a mesh axis runs over, the one named last changes fastest.
Arguments:
- keys: bfloat16 [65536, 5120], P('ctx', 'head'), may hold values from -6 to 6
- values: bfloat16 [65536, 5120], P('ctx', 'head'), may hold values from -6 to 6
- queries: bfloat16 [65536, 5120], P('ctx', 'head'), may hold values from -6 to 6
- rates: float32 [65536, 16], P('ctx', 'head'), may hold values from 9.765625e-05 to 0.0009765625
- w_gate: bfloat16 [320, 16, 320], P('ctx', 'head'), may hold values from -0.3125 to 0.3125
- w_up: bfloat16 [320, 16, 320], P('ctx', 'head'), may hold values from -0.3125 to 0.3125
- w_down: bfloat16 [320, 16, 320], P('ctx', 'head'), may hold values from -0.3125 to 0.3125
- gain: float32 [5120], P('head'), may hold values from 0.5 to 1.5
Outputs:
- output: bfloat16 [65536, 5120], P('ctx', 'head')
- new_gate: bfloat16 [320, 16, 320], P('ctx', 'head')
- new_up: bfloat16 [320, 16, 320], P('ctx', 'head')
- new_down: bfloat16 [320, 16, 320], P('ctx', 'head')
The draws below stay inside these ranges and needn't reach their ends.
All inputs are finite; a program needn't handle non-finite values.
Results may differ from the reference program's by a relative error of at most 0.0092.
Values may be sent and summed in bfloat16 or wider, within the bound.
No kernel may reach another device: no remote copies, remote signals or barrier semaphores. Data moves between devices by JAX's collectives and lax.ppermute only.
A program may use at most 128 MiB of HBM per device.

```python
import math
import jax
import jax.numpy as jnp
from jax import lax

HEADS = 16
DH = 320
FF = 320
TOKENS = 65536
WIDTH = 5120


def block_scale(own_key, extent, split, smallest, high):
    level, own = 1.0, jax.random.fold_in(own_key, 6)
    for position, parts in split:
        heights = jnp.exp(jax.random.uniform(jax.random.fold_in(own, position), (parts,), jnp.float32, smallest / len(split), high / len(split)))
        level = level * jnp.repeat(heights, extent[position] // parts).reshape([-1 if axis == position else 1 for axis in range(len(extent))])
    return level


def bell_draw(own_key, shape, spread, most, pieces=(), dtype=jnp.bfloat16):
    drawn = spread * jax.random.normal(own_key, shape, jnp.float32)
    if pieces:
        drawn = drawn * block_scale(own_key, shape, pieces, -0.22, 0.18)
    return jnp.clip(drawn, -most, most).astype(dtype)


def setup_inputs(seed: int = 0) -> dict:
    arg_keys = jax.random.split(jax.random.key(seed), 9)
    return {
        "keys": bell_draw(arg_keys[0], (TOKENS, WIDTH), 1.0, 6.0, ((0, 32), (1, 8))),
        "values": bell_draw(arg_keys[1], (TOKENS, WIDTH), 1.0, 6.0, ((0, 32), (1, 8))),
        "queries": bell_draw(arg_keys[2], (TOKENS, WIDTH), 1.0, 6.0, ((0, 32), (1, 8))),
        "rates": jnp.clip(jnp.exp(math.log(0.0009765625) - 2.3025851 * jax.random.uniform(arg_keys[3], (TOKENS, HEADS), jnp.float32) ** block_scale(arg_keys[3], (TOKENS, HEADS), ((0, 32), (1, 8)), -0.2, 0.2)), 9.765625145519152e-05, 0.0009765625),
        "w_gate": bell_draw(arg_keys[4], (FF, HEADS, DH), DH ** -0.5, 0.3125, ((0, 32), (1, 8))),
        "w_up": bell_draw(arg_keys[5], (FF, HEADS, DH), DH ** -0.5, 0.3125, ((0, 32), (1, 8))),
        "w_down": bell_draw(arg_keys[6], (FF, HEADS, DH), FF ** -0.5, 0.3125, ((0, 32), (1, 8))),
        "gain": jnp.clip(1.0 + 0.1 * jax.random.normal(arg_keys[7], (WIDTH,), jnp.float32), 0.5, 1.5),
    }


EPS = 1e-06

def renorm(weight, grad):
    old = weight.astype(jnp.float32)
    updated = old + grad
    old_sq = lax.optimization_barrier(jnp.sum(old * old, axis=0))
    new_sq = lax.optimization_barrier(jnp.sum(updated * updated, axis=0))
    return (updated * (jnp.sqrt(old_sq) * lax.rsqrt(new_sq + EPS))[None, :]).astype(jnp.bfloat16)

def update_head(operands):
    keyh, valueh, rateh, wgate, wup, wdown = operands
    gpre = jnp.dot(keyh, wgate.T, preferred_element_type=jnp.float32)
    upre = jnp.dot(keyh, wup.T, preferred_element_type=jnp.float32)
    sig = jax.nn.sigmoid(gpre)
    act = gpre * sig
    slope = sig * (1.0 + gpre * (1.0 - sig))
    hidden = (act * upre).astype(jnp.bfloat16)
    scaled = (valueh.astype(jnp.float32) * rateh[:, None]).astype(jnp.bfloat16)
    back = jnp.dot(scaled, wdown.T, preferred_element_type=jnp.float32)
    dgate = (back * upre * slope).astype(jnp.bfloat16)
    dup = (back * act).astype(jnp.bfloat16)
    grad_gate = jnp.dot(dgate.T, keyh, preferred_element_type=jnp.float32)
    grad_up = jnp.dot(dup.T, keyh, preferred_element_type=jnp.float32)
    grad_down = jnp.dot(hidden.T, scaled, preferred_element_type=jnp.float32)
    return (renorm(wgate, grad_gate), renorm(wup, grad_up), renorm(wdown, grad_down))

def apply_head(queryh, wgate, wup, wdown):
    gpre = jnp.dot(queryh, wgate.T, preferred_element_type=jnp.float32)
    upre = jnp.dot(queryh, wup.T, preferred_element_type=jnp.float32)
    mixed = (jax.nn.silu(gpre) * upre).astype(jnp.bfloat16)
    return jnp.dot(mixed, wdown, preferred_element_type=jnp.float32)

def reference(keys, values, queries, rates, w_gate, w_up, w_down, gain):
    rows = keys.shape[0]
    keyh = keys.reshape(rows, HEADS, DH).transpose(1, 0, 2)
    valueh = values.reshape(rows, HEADS, DH).transpose(1, 0, 2)
    queryh = queries.reshape(rows, HEADS, DH).transpose(1, 0, 2)
    rateh = rates.T
    new_gate, new_up, new_down = lax.map(update_head, (keyh, valueh, rateh, w_gate.transpose(1, 0, 2), w_up.transpose(1, 0, 2), w_down.transpose(1, 0, 2)))

    def head_squares(operands):
        outh = apply_head(*operands)
        return lax.optimization_barrier(jnp.sum(outh * outh, axis=1))
    squares = lax.optimization_barrier(jnp.sum(lax.map(head_squares, (queryh, new_gate, new_up, new_down)), axis=0))
    scale = lax.rsqrt(squares / (HEADS * DH) + EPS)
    gainh = gain.reshape(HEADS, DH)

    def head_output(operands):
        queryone, wgate, wup, wdown, gainone = operands
        outh = apply_head(queryone, wgate, wup, wdown)
        return (outh * scale[:, None] * gainone[None, :]).astype(jnp.bfloat16)
    output = lax.map(head_output, (queryh, new_gate, new_up, new_down, gainh))
    output = output.transpose(1, 0, 2).reshape(rows, HEADS * DH)
    return (output, new_gate.transpose(1, 0, 2), new_up.transpose(1, 0, 2), new_down.transpose(1, 0, 2))
```

```python
import jax
import jax.numpy as jnp
from jax import lax
from jax.experimental import pallas as pl
from jax.experimental.pallas import tpu as pltpu
from jax.sharding import Mesh
from jax.sharding import PartitionSpec as P

EPS = 1e-06
X, Z, Y, CORE = 4, 8, 4, 2
DH, FF, HEADS = 320, 320, 16
LOCAL = FF // (X * Z)
BLOCK = FF // X
WIN = 384
LANES = 2 * DH
F32, BF16 = jnp.float32, jnp.bfloat16
NT = (((1,), (1,)), ((), ()))


def shifted(array, axis, by):
    n = lax.axis_size(axis)
    return lax.ppermute(array, axis, [(i, (i - by) % n) for i in range(n)])


def gathered_z(rows):
    every = lax.all_to_all(jnp.broadcast_to(rows[None], (Z, *rows.shape)), "z", 0, 0, tiled=True)
    return jnp.moveaxis(every.reshape(Z, 3, LOCAL, LANES), 0, 1).reshape(3, BLOCK, LANES)


def gathered(rows):
    block = gathered_z(rows)
    return [block] + [shifted(block, "x", s) for s in (1, 2, 3)]


def own_lanes(head):
    lane = lax.broadcasted_iota(jnp.int32, (BLOCK, WIN), 1)
    return lane < DH if head == 0 else lane >= WIN - DH


def side_by_side(first, second):
    lane = lax.broadcasted_iota(jnp.int32, (first.shape[0], WIN - 256), 1)
    middle = jnp.where(lane < DH - 256, first[:, 256:], second[:, : WIN - 256])
    return jnp.concatenate([first[:, :256], middle, second[:, WIN - 256 :]], axis=1)


def update_body(k_ref, v_ref, r_ref, *refs):
    w_refs, g_refs, (osq_ref, wgu, wd, agu, ad) = refs[:X], refs[X : 2 * X], refs[2 * X :]
    step = pl.program_id(0)

    @pl.when(step == 0)
    def _():
        sq = [jnp.zeros((1, LANES), F32) for _ in range(3)]
        for b, w_ref in enumerate(w_refs):
            for m in range(3):
                w = w_ref[m]
                wf = w.astype(F32)
                sq[m] += jnp.sum(wf * wf, axis=0, keepdims=True)
                for h in range(2):
                    part = jnp.where(own_lanes(h), w[:, h * 256 : h * 256 + WIN], jnp.zeros((), BF16))
                    if m < 2:
                        wgu[h, pl.ds(m * FF + b * BLOCK, BLOCK), :] = part
                    else:
                        wd[h, pl.ds(b * BLOCK, BLOCK), :] = part
        for m in range(3):
            osq_ref[m : m + 1, :] = sq[m]
        agu[...] = jnp.zeros_like(agu)
        ad[...] = jnp.zeros_like(ad)

    for h in range(2):
        k = k_ref[:, h * 256 : h * 256 + WIN]
        v = v_ref[:, h * 256 : h * 256 + WIN]
        rate = r_ref[h : h + 1, :]
        gu = lax.dot_general(wgu[h], k, NT, preferred_element_type=F32)
        back = lax.dot_general(wd[h], v, NT, preferred_element_type=F32) * rate
        g, u = gu[:FF], gu[FF:]
        s = 0.5 * jnp.tanh(0.5 * g) + 0.5
        act = g * s
        slope = s + act * (1.0 - s)
        dgate = (back * u * slope).astype(BF16)
        dup = (back * act).astype(BF16)
        hidden = (act * u * rate).astype(BF16)
        agu[h] += jnp.dot(jnp.concatenate([dgate, dup], axis=0), k, preferred_element_type=F32)
        ad[h] += jnp.dot(hidden, v, preferred_element_type=F32)

    @pl.when(step == pl.num_programs(0) - 1)
    def _():
        for b, g_ref in enumerate(g_refs):
            for m in range(3):
                acc, at = (agu, m * FF + b * BLOCK) if m < 2 else (ad, b * BLOCK)
                rows = pl.ds(at, BLOCK)
                g_ref[m] = side_by_side(acc[0, rows, :], acc[1, rows, :]).astype(BF16)


def update(keys, values, rates, blocks, tile=512):
    tokens = keys.shape[0]
    whole = pl.BlockSpec((3, BLOCK, LANES), lambda i: (0, 0, 0))
    rowspec = pl.BlockSpec((tile, LANES), lambda i: (i, 0))
    outs = pl.pallas_call(
        update_body,
        grid=(tokens // tile,),
        in_specs=[rowspec, rowspec, pl.BlockSpec((2, tile), lambda i: (0, i))] + [whole] * X,
        out_specs=[whole] * X + [pl.BlockSpec((3, LANES), lambda i: (0, 0))],
        out_shape=[jax.ShapeDtypeStruct((3, BLOCK, LANES), BF16)] * X + [jax.ShapeDtypeStruct((3, LANES), F32)],
        scratch_shapes=[
            pltpu.VMEM((2, 2 * FF, WIN), BF16),
            pltpu.VMEM((2, FF, WIN), BF16),
            pltpu.VMEM((2, 2 * FF, WIN), F32),
            pltpu.VMEM((2, FF, WIN), F32),
        ],
        cost_estimate=pl.CostEstimate(
            flops=24 * tokens * FF * WIN, bytes_accessed=4 * tokens * LANES, transcendentals=2 * tokens * FF
        ),
        name="update",
    )(keys, values, rates, *blocks)
    return outs[:X], outs[X]


def apply_body(q_ref, osq_ref, *refs):
    u_refs, (o_ref, sq_ref, sc_ref, wgu, wd) = refs[:X], refs[X:]

    @pl.when(pl.program_id(0) == 0)
    def _():
        wgu[...] = jnp.zeros_like(wgu)
        wd[...] = jnp.zeros_like(wd)
        for m in range(3):
            sq = jnp.zeros((1, LANES), F32)
            for u_ref in u_refs:
                wf = u_ref[m].astype(F32)
                sq += jnp.sum(wf * wf, axis=0, keepdims=True)
            sc = jnp.sqrt(osq_ref[m : m + 1, :]) * lax.rsqrt(sq + EPS)
            sc_ref[m : m + 1, :] = sc
            for b, u_ref in enumerate(u_refs):
                for h in range(2):
                    cols = slice(h * 256, h * 256 + WIN)
                    if m < 2:
                        part = (u_ref[m, :, cols].astype(F32) * sc[:, cols]).astype(BF16)
                        part = jnp.where(own_lanes(h), part, jnp.zeros((), BF16))
                        wgu[h, pl.ds(m * WIN + b * BLOCK, BLOCK), :] = part
                    else:
                        wd[h, pl.ds(b * BLOCK, BLOCK), :] = u_ref[m, :, cols]

    outs = []
    for h in range(2):
        q = q_ref[:, h * 256 : h * 256 + WIN]
        gu = lax.dot_general(q, wgu[h], NT, preferred_element_type=F32)
        g, u = gu[:, :WIN], gu[:, WIN:]
        mixed = (g * (0.5 * jnp.tanh(0.5 * g) + 0.5) * u).astype(BF16)
        outs.append(jnp.dot(mixed, wd[h], preferred_element_type=F32))
    o = side_by_side(*outs) * sc_ref[2:3, :]
    o_ref[...] = o
    ones = jnp.ones((8, LANES), F32)
    sq_ref[...] = lax.dot_general(ones, o * o, NT, preferred_element_type=F32)[:1]


def apply(queries, old_sq, blocks, tile=512):
    tokens = queries.shape[0]
    whole = pl.BlockSpec((3, BLOCK, LANES), lambda i: (0, 0, 0))
    small = pl.BlockSpec((3, LANES), lambda i: (0, 0))
    return pl.pallas_call(
        apply_body,
        grid=(tokens // tile,),
        in_specs=[pl.BlockSpec((tile, LANES), lambda i: (i, 0)), small] + [whole] * X,
        out_specs=[
            pl.BlockSpec((tile, LANES), lambda i: (i, 0)),
            pl.BlockSpec((1, tile), lambda i: (0, i)),
            small,
        ],
        out_shape=[
            jax.ShapeDtypeStruct((tokens, LANES), F32),
            jax.ShapeDtypeStruct((1, tokens), F32),
            jax.ShapeDtypeStruct((3, LANES), F32),
        ],
        scratch_shapes=[pltpu.VMEM((2, 2 * WIN, WIN), BF16), pltpu.VMEM((2, WIN, WIN), BF16)],
        cost_estimate=pl.CostEstimate(
            flops=12 * tokens * FF * WIN, bytes_accessed=6 * tokens * LANES, transcendentals=2 * tokens * FF
        ),
        name="apply",
    )(queries, old_sq, *blocks)


def scale_body(o_ref, sq_ref, gain_ref, out_ref):
    gain = gain_ref[...]
    for j in range(o_ref.shape[0] // 128):
        rows = pl.ds(j * 128, 128)
        scale = lax.rsqrt(sq_ref[:, rows] / (HEADS * DH) + EPS)
        across = jnp.transpose(jnp.broadcast_to(scale, (128, 128)))
        for c in range(LANES // 128):
            cols = slice(c * 128, (c + 1) * 128)
            out_ref[rows, cols] = (o_ref[rows, cols] * across * gain[:, cols]).astype(BF16)


def scaled_output(o, squares, gain, tile=512):
    tokens = o.shape[0]
    rowspec = pl.BlockSpec((tile, LANES), lambda i: (i, 0))
    return pl.pallas_call(
        scale_body,
        grid=(tokens // tile,),
        in_specs=[rowspec, pl.BlockSpec((1, tile), lambda i: (0, i)), pl.BlockSpec((1, LANES), lambda i: (0, 0))],
        out_specs=rowspec,
        out_shape=jax.ShapeDtypeStruct((tokens, LANES), BF16),
        name="scale",
    )(o, squares, gain)


def per_device(keys, values, queries, rates, w_gate, w_up, w_down, gain):
    own = jnp.stack([w.reshape(LOCAL, LANES) for w in (w_gate, w_up, w_down)]).reshape(3 * LOCAL, LANES)
    grads, old_sq = update(keys, values, rates.T, gathered(own))

    total = grads[0].astype(F32)
    for s in (1, 2, 3):
        total += shifted(grads[s], "x", -s).astype(F32)
    pieces = jnp.moveaxis(total.astype(BF16).reshape(3, Z, LOCAL, LANES), 1, 0).reshape(Z, 3 * LOCAL, LANES)
    pieces = lax.all_to_all(pieces, "z", 0, 0, tiled=True)
    updated = own.astype(F32) + jnp.sum(pieces.astype(F32), axis=0)

    o, squares, scale = apply(queries, old_sq, gathered(updated.astype(BF16)))
    squares += shifted(squares, "core", 1)
    squares = squares + shifted(squares, "y", 1) + shifted(squares, "y", 2) + shifted(squares, "y", 3)
    output = scaled_output(o, squares, gain.reshape(1, LANES))
    fresh = (updated.reshape(3, LOCAL, LANES) * scale[:, None, :]).astype(BF16).reshape(3, LOCAL, 2, DH)
    return output, fresh[0], fresh[1], fresh[2]


def solution(mesh):
    split = Mesh(mesh.devices.reshape(X, Z, Y, CORE), ("x", "z", "y", "core"))
    ctx, head = ("x", "z"), ("y", "core")
    weight = P(ctx, head, None)
    return jax.shard_map(
        per_device,
        mesh=split,
        in_specs=(P(ctx, head),) * 4 + (weight,) * 3 + (P(head),),
        out_specs=(P(ctx, head),) + (weight,) * 3,
        check_vma=False,
    )
```

```python
import functools

import jax
import jax.numpy as jnp
from jax import lax
from jax.experimental import pallas as pl
from jax.experimental.pallas import tpu as pltpu
from jax.sharding import Mesh
from jax.sharding import PartitionSpec as P

EPS = 1e-06
X, Z, Y, CORE = 4, 8, 4, 2
DH, FF, HEADS = 320, 320, 16
LOCAL = FF // (X * Z)
BLOCK = FF // X
WIN = 384
LANES = 2 * DH
VMEM = 28 << 20
F32, BF16 = jnp.float32, jnp.bfloat16
NT = (((1,), (1,)), ((), ()))


def shifted(array, axis, by):
    n = lax.axis_size(axis)
    return lax.ppermute(array, axis, [(i, (i - by) % n) for i in range(n)])


def gathered_z(copies):
    every = lax.all_to_all(copies, "z", 0, 0, tiled=True)
    return jnp.moveaxis(every.reshape(Z, 3, LOCAL, LANES), 0, 1).reshape(3, BLOCK, LANES)


def in_turn(value, *first):
    return lax.optimization_barrier((value, *first))[0]


def own_lanes(head):
    lane = lax.broadcasted_iota(jnp.int32, (BLOCK, WIN), 1)
    return lane < DH if head == 0 else lane >= WIN - DH


def side_by_side(first, second):
    lane = lax.broadcasted_iota(jnp.int32, (first.shape[0], WIN - 256), 1)
    middle = jnp.where(lane < DH - 256, first[:, 256:], second[:, : WIN - 256])
    return jnp.concatenate([first[:, :256], middle, second[:, WIN - 256 :]], axis=1)


def update_body(blocks, k_ref, v_ref, r_ref, *refs):
    w_refs, g_refs, (osq_ref, wgu, wd, agu, ad) = refs[:blocks], refs[blocks : 2 * blocks], refs[2 * blocks :]
    step = pl.program_id(0)
    units = blocks * BLOCK

    @pl.when(step == 0)
    def _():
        sq = [jnp.zeros((1, LANES), F32) for _ in range(3)]
        for b, w_ref in enumerate(w_refs):
            for m in range(3):
                w = w_ref[m]
                wf = w.astype(F32)
                sq[m] += jnp.sum(wf * wf, axis=0, keepdims=True)
                for h in range(2):
                    part = jnp.where(own_lanes(h), w[:, h * 256 : h * 256 + WIN], jnp.zeros((), BF16))
                    if m < 2:
                        wgu[h, pl.ds(m * units + b * BLOCK, BLOCK), :] = part
                    else:
                        wd[h, pl.ds(b * BLOCK, BLOCK), :] = part
        for m in range(3):
            osq_ref[m : m + 1, :] = sq[m]
        agu[...] = jnp.zeros_like(agu)
        ad[...] = jnp.zeros_like(ad)

    for h in range(2):
        k = k_ref[:, h * 256 : h * 256 + WIN]
        v = v_ref[:, h * 256 : h * 256 + WIN]
        rate = r_ref[h : h + 1, :]
        gu = lax.dot_general(wgu[h], k, NT, preferred_element_type=F32)
        back = lax.dot_general(wd[h], v, NT, preferred_element_type=F32) * rate
        g, u = gu[:units], gu[units:]
        s = 0.5 * jnp.tanh(0.5 * g) + 0.5
        act = g * s
        slope = s + act * (1.0 - s)
        dgate = (back * u * slope).astype(BF16)
        dup = (back * act).astype(BF16)
        hidden = (act * u * rate).astype(BF16)
        agu[h] += jnp.dot(jnp.concatenate([dgate, dup], axis=0), k, preferred_element_type=F32)
        ad[h] += jnp.dot(hidden, v, preferred_element_type=F32)

    @pl.when(step == pl.num_programs(0) - 1)
    def _():
        for b, g_ref in enumerate(g_refs):
            for m in range(3):
                acc, at = (agu, m * units + b * BLOCK) if m < 2 else (ad, b * BLOCK)
                rows = pl.ds(at, BLOCK)
                g_ref[m] = side_by_side(acc[0, rows, :], acc[1, rows, :]).astype(BF16)


def update(keys, values, rates, blocks, tile=1024):
    tokens, n = keys.shape[0], len(blocks)
    whole = pl.BlockSpec((3, BLOCK, LANES), lambda i: (0, 0, 0))
    rowspec = pl.BlockSpec((tile, LANES), lambda i: (i, 0))
    outs = pl.pallas_call(
        functools.partial(update_body, n),
        grid=(tokens // tile,),
        in_specs=[rowspec, rowspec, pl.BlockSpec((2, tile), lambda i: (0, i))] + [whole] * n,
        out_specs=[whole] * n + [pl.BlockSpec((3, LANES), lambda i: (0, 0))],
        out_shape=[jax.ShapeDtypeStruct((3, BLOCK, LANES), BF16)] * n + [jax.ShapeDtypeStruct((3, LANES), F32)],
        scratch_shapes=[
            pltpu.VMEM((2, 2 * n * BLOCK, WIN), BF16),
            pltpu.VMEM((2, n * BLOCK, WIN), BF16),
            pltpu.VMEM((2, 2 * n * BLOCK, WIN), F32),
            pltpu.VMEM((2, n * BLOCK, WIN), F32),
        ],
        cost_estimate=pl.CostEstimate(
            flops=48 * tokens * n * BLOCK * WIN, bytes_accessed=4 * tokens * LANES, transcendentals=2 * tokens * FF
        ),
        compiler_params=pltpu.CompilerParams(vmem_limit_bytes=VMEM),
        name="update",
    )(keys, values, rates, *blocks)
    return outs[:n], outs[n]


def apply_body(part, q_ref, osq_ref, *refs):
    u_refs, (o_ref, sq_ref, sc_ref, wgu, wd) = refs[:X], refs[X:]

    @pl.when(pl.program_id(0) == 0)
    def _():
        wgu[...] = jnp.zeros_like(wgu)
        wd[...] = jnp.zeros_like(wd)
        for m in range(3):
            sq = jnp.zeros((1, LANES), F32)
            for u_ref in u_refs:
                wf = u_ref[m].astype(F32)
                sq += jnp.sum(wf * wf, axis=0, keepdims=True)
            sc = jnp.sqrt(osq_ref[m : m + 1, :]) * lax.rsqrt(sq + EPS)
            sc_ref[m : m + 1, :] = sc
            for b, u_ref in enumerate(u_refs):
                for h in range(2):
                    cols = slice(h * 256, h * 256 + WIN)
                    if m < 2:
                        part = (u_ref[m, :, cols].astype(F32) * sc[:, cols]).astype(BF16)
                        part = jnp.where(own_lanes(h), part, jnp.zeros((), BF16))
                        wgu[h, pl.ds(m * WIN + b * BLOCK, BLOCK), :] = part
                    else:
                        wd[h, pl.ds(b * BLOCK, BLOCK), :] = u_ref[m, :, cols]

    def project(rows, h):
        q = q_ref[rows, h * 256 : h * 256 + WIN]
        return lax.dot_general(q, wgu[h], NT, preferred_element_type=F32)

    def finish(rows, outs):
        o = side_by_side(*outs) * sc_ref[2:3, :]
        o_ref[rows, :] = o
        sq = o * o
        sq = sum(sq[:, c * 128 : (c + 1) * 128] for c in range(1, LANES // 128)) + sq[:, :128]
        for j in range(o.shape[0] // 128):
            at = rows.start // 128 + j
            sq_ref[at : at + 1, :] = jnp.sum(jnp.transpose(sq[j * 128 : (j + 1) * 128]), axis=0, keepdims=True)

    steps = [(slice(r, r + part), h) for r in range(0, q_ref.shape[0], part) for h in range(2)]
    ahead, outs = project(*steps[0]), []
    for i, (rows, h) in enumerate(steps):
        g, u = ahead[:, :WIN], ahead[:, WIN:]
        if i + 1 < len(steps):
            ahead = project(*steps[i + 1])
        mixed = (g * (0.5 * jnp.tanh(0.5 * g) + 0.5) * u).astype(BF16)
        outs.append(jnp.dot(mixed, wd[h], preferred_element_type=F32))
        if h == 1:
            finish(rows, outs)
            outs = []


def apply(queries, old_sq, blocks, tile=1024, part=512):
    tokens = queries.shape[0]
    whole = pl.BlockSpec((3, BLOCK, LANES), lambda i: (0, 0, 0))
    small = pl.BlockSpec((3, LANES), lambda i: (0, 0))
    return pl.pallas_call(
        functools.partial(apply_body, part),
        grid=(tokens // tile,),
        in_specs=[pl.BlockSpec((tile, LANES), lambda i: (i, 0)), small] + [whole] * X,
        out_specs=[
            pl.BlockSpec((tile, LANES), lambda i: (i, 0)),
            pl.BlockSpec((tile // 128, 128), lambda i: (i, 0)),
            small,
        ],
        out_shape=[
            pltpu.HBM((tokens, LANES), F32),
            jax.ShapeDtypeStruct((tokens // 128, 128), F32),
            jax.ShapeDtypeStruct((3, LANES), F32),
        ],
        scratch_shapes=[pltpu.VMEM((2, 2 * WIN, WIN), BF16), pltpu.VMEM((2, WIN, WIN), BF16)],
        cost_estimate=pl.CostEstimate(
            flops=12 * tokens * FF * WIN, bytes_accessed=6 * tokens * LANES, transcendentals=2 * tokens * FF
        ),
        compiler_params=pltpu.CompilerParams(vmem_limit_bytes=VMEM),
        name="apply",
    )(queries, old_sq, *blocks)


def scale_body(o_ref, gain_ref, *refs):
    sq_refs, out_ref = refs[:-1], refs[-1]
    gain = gain_ref[...]
    sq = sum(r[...] for r in sq_refs[1:]) + sq_refs[0][...]
    scale = lax.rsqrt(sq / (HEADS * DH) + EPS)
    for j in range(o_ref.shape[0] // 128):
        rows = pl.ds(j * 128, 128)
        across = jnp.transpose(jnp.broadcast_to(scale[j : j + 1], (128, 128)))
        for c in range(LANES // 128):
            cols = slice(c * 128, (c + 1) * 128)
            out_ref[rows, cols] = (o_ref[rows, cols] * across * gain[:, cols]).astype(BF16)


def scaled_output(o, squares, gain, tile=1024):
    tokens = o.shape[0]
    rowspec = pl.BlockSpec((tile, LANES), lambda i: (i, 0))
    sqspec = pl.BlockSpec((tile // 128, 128), lambda i: (i, 0))
    return pl.pallas_call(
        scale_body,
        grid=(tokens // tile,),
        in_specs=[rowspec, pl.BlockSpec((1, LANES), lambda i: (0, 0))] + [sqspec] * len(squares),
        out_specs=rowspec,
        out_shape=jax.ShapeDtypeStruct((tokens, LANES), BF16),
        compiler_params=pltpu.CompilerParams(vmem_limit_bytes=VMEM),
        name="scale",
    )(o, gain, *squares)


def pack_body(gate_ref, up_ref, down_ref, own_ref, copies_ref):
    rows = []
    for w_ref in (gate_ref, up_ref, down_ref):
        w = w_ref[...].astype(F32)
        rows.append(jnp.concatenate([w[:, 0, :], w[:, 1, :]], axis=1))
    own = jnp.concatenate(rows, axis=0).astype(BF16)
    own_ref[...] = own
    for z in range(Z):
        copies_ref[z] = own


def packed(weights):
    return pl.pallas_call(
        pack_body,
        out_shape=[
            jax.ShapeDtypeStruct((3 * LOCAL, LANES), BF16),
            jax.ShapeDtypeStruct((Z, 3 * LOCAL, LANES), BF16),
        ],
        name="pack",
    )(*weights)


def per_device(keys, values, queries, rates, w_gate, w_up, w_down, gain):
    own, copies = packed((w_gate, w_up, w_down))
    rates = rates.T
    here = gathered_z(copies)
    across = shifted(here, "x", 2)
    sides = shifted(here, "x", 1), shifted(here, "x", 3)
    (g0,), sq_a = update(keys, values, rates, (here,))
    (g2,), sq_b = update(keys, values, in_turn(rates, g0), (across,))
    r2 = shifted(g2, "x", 2)
    (g1, g3), sq_c = update(keys, values, in_turn(rates, g2), sides)
    r1, r3 = shifted(g1, "x", 3), shifted(g3, "x", 1)
    total = lax.optimization_barrier(g0.astype(F32) + r2.astype(F32)) + r1.astype(F32) + r3.astype(F32)
    old_sq = sq_a + sq_b + sq_c
    pieces = jnp.moveaxis(total.astype(BF16).reshape(3, Z, LOCAL, LANES), 1, 0).reshape(Z, 3 * LOCAL, LANES)
    pieces = lax.all_to_all(pieces, "z", 0, 0, tiled=True)
    updated = own.astype(F32) + jnp.sum(pieces.astype(F32), axis=0)

    here = gathered_z(jnp.broadcast_to(updated.astype(BF16)[None], (Z, 3 * LOCAL, LANES)))
    new = [here] + [shifted(here, "x", s) for s in (1, 3, 2)]
    o, squares, scale = apply(queries, old_sq, new)
    squares = squares.reshape(-1)
    squares += shifted(squares, "core", 1)
    squares = [squares] + [shifted(squares, "y", s) for s in (2, 1, 3)]
    o = pltpu.with_memory_space_constraint(o, pltpu.HBM)
    output = scaled_output(o, [s.reshape(-1, 128) for s in squares], gain.reshape(1, LANES))
    fresh = (updated.reshape(3, LOCAL, LANES) * scale[:, None, :]).astype(BF16).reshape(3, LOCAL, 2, DH)
    return output, fresh[0], fresh[1], fresh[2]


def solution(mesh):
    split = Mesh(mesh.devices.reshape(X, Z, Y, CORE), ("x", "z", "y", "core"))
    ctx, head = ("x", "z"), ("y", "core")
    weight = P(ctx, head, None)
    return jax.shard_map(
        per_device,
        mesh=split,
        in_specs=(P(ctx, head),) * 4 + (weight,) * 3 + (P(head),),
        out_specs=(P(ctx, head),) + (weight,) * 3,
        check_vma=False,
    )
```

```python
import functools

import jax
import jax.numpy as jnp
from jax import lax
from jax.experimental import pallas as pl
from jax.experimental.pallas import tpu as pltpu
from jax.sharding import Mesh
from jax.sharding import PartitionSpec as P

EPS = 1e-06
X, Z, Y, CORE = 4, 8, 4, 2
DH, FF, HEADS = 320, 320, 16
LOCAL = FF // (X * Z)
BLOCK = FF // X
WIN = 384
LANES = 2 * DH
VMEM = 28 << 20
F32, BF16 = jnp.float32, jnp.bfloat16
NT = (((1,), (1,)), ((), ()))


def shifted(array, axis, by):
    n = lax.axis_size(axis)
    return lax.ppermute(array, axis, [(i, (i - by) % n) for i in range(n)])


def gathered_z(copies):
    every = lax.all_to_all(copies, "z", 0, 0, tiled=True)
    return jnp.moveaxis(every.reshape(Z, 3, LOCAL, LANES), 0, 1).reshape(3, BLOCK, LANES)


def in_turn(value, *first):
    return lax.optimization_barrier((value, *first))[0]


def own_lanes(head):
    lane = lax.broadcasted_iota(jnp.int32, (BLOCK, WIN), 1)
    return lane < DH if head == 0 else lane >= WIN - DH


def side_by_side(first, second):
    lane = lax.broadcasted_iota(jnp.int32, (first.shape[0], WIN - 256), 1)
    middle = jnp.where(lane < DH - 256, first[:, 256:], second[:, : WIN - 256])
    return jnp.concatenate([first[:, :256], middle, second[:, WIN - 256 :]], axis=1)


def update_body(blocks, tile, k_ref, v_ref, r_ref, *refs):
    w_refs, g_refs, (osq_ref, wgu, wd, agu, ad) = refs[:blocks], refs[blocks : 2 * blocks], refs[2 * blocks :]
    units = blocks * BLOCK
    sq = [jnp.zeros((1, LANES), F32) for _ in range(3)]
    for b, w_ref in enumerate(w_refs):
        for m in range(3):
            w = w_ref[m]
            wf = w.astype(F32)
            sq[m] += jnp.sum(wf * wf, axis=0, keepdims=True)
            for h in range(2):
                part = jnp.where(own_lanes(h), w[:, h * 256 : h * 256 + WIN], jnp.zeros((), BF16))
                if m < 2:
                    wgu[h, pl.ds(m * units + b * BLOCK, BLOCK), :] = part
                else:
                    wd[h, pl.ds(b * BLOCK, BLOCK), :] = part
    for m in range(3):
        osq_ref[m : m + 1, :] = sq[m]

    for at in range(0, k_ref.shape[0], tile):
        for h in range(2):
            k = k_ref[at : at + tile, h * 256 : h * 256 + WIN]
            v = v_ref[at : at + tile, h * 256 : h * 256 + WIN]
            rate = r_ref[h : h + 1, at : at + tile]
            gu = lax.dot_general(wgu[h], k, NT, preferred_element_type=F32)
            back = lax.dot_general(wd[h], v, NT, preferred_element_type=F32) * rate
            g, u = gu[:units], gu[units:]
            s = 0.5 * jnp.tanh(0.5 * g) + 0.5
            act = g * s
            slope = s + act * (1.0 - s)
            dgate = (back * u * slope).astype(BF16)
            dup = (back * act).astype(BF16)
            hidden = (act * u * rate).astype(BF16)
            ggu = jnp.dot(jnp.concatenate([dgate, dup], axis=0), k, preferred_element_type=F32)
            gd = jnp.dot(hidden, v, preferred_element_type=F32)
            agu[h] = ggu if at == 0 else agu[h] + ggu
            ad[h] = gd if at == 0 else ad[h] + gd

    for b, g_ref in enumerate(g_refs):
        for m in range(3):
            acc, at = (agu, m * units + b * BLOCK) if m < 2 else (ad, b * BLOCK)
            rows = pl.ds(at, BLOCK)
            g_ref[m] = side_by_side(acc[0, rows, :], acc[1, rows, :]).astype(BF16)


def update(keys, values, rates, blocks, tile=1024):
    tokens, n = keys.shape[0], len(blocks)
    vmem = pl.BlockSpec(memory_space=pltpu.VMEM)
    outs = pl.pallas_call(
        functools.partial(update_body, n, tile),
        in_specs=[vmem] * (3 + n),
        out_specs=[vmem] * (n + 1),
        out_shape=[jax.ShapeDtypeStruct((3, BLOCK, LANES), BF16)] * n + [jax.ShapeDtypeStruct((3, LANES), F32)],
        scratch_shapes=[
            pltpu.VMEM((2, 2 * n * BLOCK, WIN), BF16),
            pltpu.VMEM((2, n * BLOCK, WIN), BF16),
            pltpu.VMEM((2, 2 * n * BLOCK, WIN), F32),
            pltpu.VMEM((2, n * BLOCK, WIN), F32),
        ],
        cost_estimate=pl.CostEstimate(
            flops=48 * tokens * n * BLOCK * WIN, bytes_accessed=4 * tokens * LANES, transcendentals=2 * tokens * FF
        ),
        compiler_params=pltpu.CompilerParams(vmem_limit_bytes=VMEM),
        name="update",
    )(keys, values, rates, *blocks)
    return outs[:n], outs[n]


def apply_body(part, q_in, osq_ref, *refs):
    u_in, (o_ref, sq_ref, sc_ref, wgu, wd, q_ref, u_refs, q_sems, u_sems) = refs[:X], refs[X:]
    tokens = q_in.shape[0]
    fetches = [pltpu.make_async_copy(u, u_refs.at[b], u_sems.at[b]) for b, u in enumerate(u_in)]
    reads = [
        pltpu.make_async_copy(q_in.at[r : r + part, :], q_ref.at[r : r + part, :], q_sems.at[r // part])
        for r in range(0, tokens, part)
    ]
    for copy in fetches + reads:
        copy.start()
    wgu[:, FF:WIN, :] = jnp.zeros((2, WIN - FF, WIN), BF16)
    wgu[:, WIN + FF :, :] = jnp.zeros((2, WIN - FF, WIN), BF16)
    wd[:, FF:, :] = jnp.zeros((2, WIN - FF, WIN), BF16)
    for fetch in fetches:
        fetch.wait()
    for m in range(3):
        sq = jnp.zeros((1, LANES), F32)
        for b in range(X):
            wf = u_refs[b, m].astype(F32)
            sq += jnp.sum(wf * wf, axis=0, keepdims=True)
        sc = jnp.sqrt(osq_ref[m : m + 1, :]) * lax.rsqrt(sq + EPS)
        sc_ref[m : m + 1, :] = sc
        for b in range(X):
            for h in range(2):
                cols = slice(h * 256, h * 256 + WIN)
                if m < 2:
                    scaled = (u_refs[b, m, :, cols].astype(F32) * sc[:, cols]).astype(BF16)
                    scaled = jnp.where(own_lanes(h), scaled, jnp.zeros((), BF16))
                    wgu[h, pl.ds(m * WIN + b * BLOCK, BLOCK), :] = scaled
                else:
                    wd[h, pl.ds(b * BLOCK, BLOCK), :] = u_refs[b, m, :, cols]
    down = sc_ref[2:3, :]

    def project(rows, h):
        if h == 0:
            reads[rows.start // part].wait()
        q = q_ref[rows, h * 256 : h * 256 + WIN]
        return lax.dot_general(q, wgu[h], NT, preferred_element_type=F32)

    def finish(rows, outs):
        o = side_by_side(*outs) * down
        o_ref[rows, :] = o.astype(BF16)
        sq = o * o
        sq = sum(sq[:, c * 128 : (c + 1) * 128] for c in range(1, LANES // 128)) + sq[:, :128]
        for j in range(o.shape[0] // 128):
            at = rows.start // 128 + j
            sq_ref[at : at + 1, :] = jnp.sum(jnp.transpose(sq[j * 128 : (j + 1) * 128]), axis=0, keepdims=True)

    steps = [(slice(r, r + part), h) for r in range(0, tokens, part) for h in range(2)]
    ahead, outs = project(*steps[0]), []
    for i, (rows, h) in enumerate(steps):
        g, u = ahead[:, :WIN], ahead[:, WIN:]
        if i + 1 < len(steps):
            ahead = project(*steps[i + 1])
        mixed = (g * (0.5 * jnp.tanh(0.5 * g) + 0.5) * u).astype(BF16)
        outs.append(jnp.dot(mixed, wd[h], preferred_element_type=F32))
        if h == 1:
            finish(rows, outs)
            outs = []


def apply(queries, old_sq, blocks, part=512):
    tokens = queries.shape[0]
    vmem, hbm = pl.BlockSpec(memory_space=pltpu.VMEM), pl.BlockSpec(memory_space=pltpu.HBM)
    return pl.pallas_call(
        functools.partial(apply_body, part),
        in_specs=[hbm, vmem] + [hbm] * X,
        out_specs=[vmem] * 3,
        out_shape=[
            jax.ShapeDtypeStruct((tokens, LANES), BF16),
            jax.ShapeDtypeStruct((tokens // 128, 128), F32),
            jax.ShapeDtypeStruct((3, LANES), F32),
        ],
        scratch_shapes=[
            pltpu.VMEM((2, 2 * WIN, WIN), BF16),
            pltpu.VMEM((2, WIN, WIN), BF16),
            pltpu.VMEM((tokens, LANES), BF16),
            pltpu.VMEM((X, 3, BLOCK, LANES), BF16),
            pltpu.SemaphoreType.DMA((tokens // part,)),
            pltpu.SemaphoreType.DMA((X,)),
        ],
        cost_estimate=pl.CostEstimate(
            flops=12 * tokens * FF * WIN, bytes_accessed=6 * tokens * LANES, transcendentals=2 * tokens * FF
        ),
        compiler_params=pltpu.CompilerParams(vmem_limit_bytes=VMEM),
        name="apply",
    )(queries, old_sq, *blocks)


def scale_body(part, o_ref, gain_ref, *refs):
    sq_refs, (out_ref, out_vmem, sems) = refs[:X], refs[X:]
    spans = [slice(r, r + part) for r in range(0, o_ref.shape[0], part)]
    gain = gain_ref[...]
    sq = sum(r[...] for r in sq_refs[1:]) + sq_refs[0][...]
    scale = lax.rsqrt(sq / (HEADS * DH) + EPS)
    writes = []
    for i, span in enumerate(spans):
        for at in range(span.start, span.stop, 128):
            rows = slice(at, at + 128)
            across = jnp.transpose(jnp.broadcast_to(scale[at // 128 : at // 128 + 1], (128, 128)))
            for c in range(LANES // 128):
                cols = slice(c * 128, (c + 1) * 128)
                out_vmem[rows, cols] = (o_ref[rows, cols].astype(F32) * across * gain[:, cols]).astype(BF16)
        write = pltpu.make_async_copy(out_vmem.at[span, :], out_ref.at[span, :], sems.at[i])
        write.start()
        writes.append(write)
    for write in writes:
        write.wait()


def scaled_output(o, squares, gain, part=256):
    tokens = o.shape[0]
    vmem, hbm = pl.BlockSpec(memory_space=pltpu.VMEM), pl.BlockSpec(memory_space=pltpu.HBM)
    return pl.pallas_call(
        functools.partial(scale_body, part),
        in_specs=[vmem] * (2 + len(squares)),
        out_specs=hbm,
        out_shape=jax.ShapeDtypeStruct((tokens, LANES), BF16),
        scratch_shapes=[
            pltpu.VMEM((tokens, LANES), BF16),
            pltpu.SemaphoreType.DMA((tokens // part,)),
        ],
        compiler_params=pltpu.CompilerParams(vmem_limit_bytes=VMEM),
        name="scale",
    )(o, gain, *squares)


def pack_body(gate_ref, up_ref, down_ref, own_ref, copies_ref):
    rows = []
    for w_ref in (gate_ref, up_ref, down_ref):
        w = w_ref[...].astype(F32)
        rows.append(jnp.concatenate([w[:, 0, :], w[:, 1, :]], axis=1))
    own = jnp.concatenate(rows, axis=0).astype(BF16)
    own_ref[...] = own
    for z in range(Z):
        copies_ref[z] = own


def packed(weights):
    return pl.pallas_call(
        pack_body,
        out_shape=[
            jax.ShapeDtypeStruct((3 * LOCAL, LANES), BF16),
            jax.ShapeDtypeStruct((Z, 3 * LOCAL, LANES), BF16),
        ],
        name="pack",
    )(*weights)


def per_device(keys, values, queries, rates, w_gate, w_up, w_down, gain):
    own, copies = packed((w_gate, w_up, w_down))
    rates = rates.T
    here = gathered_z(copies)
    across = shifted(here, "x", 2)
    sides = shifted(here, "x", 1), shifted(here, "x", 3)
    (g0,), sq_a = update(keys, values, rates, (here,))
    (g2,), sq_b = update(keys, values, in_turn(rates, g0), (across,))
    r2 = shifted(g2, "x", 2)
    (g1, g3), sq_c = update(keys, values, in_turn(rates, g2), sides)
    r1, r3 = shifted(g1, "x", 3), shifted(g3, "x", 1)
    total = lax.optimization_barrier(g0.astype(F32) + r2.astype(F32)) + r1.astype(F32) + r3.astype(F32)
    old_sq = sq_a + sq_b + sq_c
    pieces = jnp.moveaxis(total.astype(BF16).reshape(3, Z, LOCAL, LANES), 1, 0).reshape(Z, 3 * LOCAL, LANES)
    pieces = lax.all_to_all(pieces, "z", 0, 0, tiled=True)
    updated = own.astype(F32) + jnp.sum(pieces.astype(F32), axis=0)

    here = gathered_z(jnp.broadcast_to(updated.astype(BF16)[None], (Z, 3 * LOCAL, LANES)))
    new = [here] + [shifted(here, "x", s) for s in (1, 3, 2)]
    queries, *new[1:3] = (pltpu.with_memory_space_constraint(a, pltpu.HBM) for a in (queries, *new[1:3]))
    o, squares, scale = apply(queries, old_sq, new)
    squares = squares.reshape(-1)
    squares += shifted(squares, "core", 1)
    squares = [squares] + [shifted(squares, "y", s) for s in (2, 1, 3)]
    output = scaled_output(o, [s.reshape(-1, 128) for s in squares], gain.reshape(1, LANES))
    fresh = (updated.reshape(3, LOCAL, LANES) * scale[:, None, :]).astype(BF16).reshape(3, LOCAL, 2, DH)
    return output, fresh[0], fresh[1], fresh[2]


def solution(mesh):
    split = Mesh(mesh.devices.reshape(X, Z, Y, CORE), ("x", "z", "y", "core"))
    ctx, head = ("x", "z"), ("y", "core")
    weight = P(ctx, head, None)
    return jax.shard_map(
        per_device,
        mesh=split,
        in_specs=(P(ctx, head),) * 4 + (weight,) * 3 + (P(head),),
        out_specs=(P(ctx, head),) + (weight,) * 3,
        check_vma=False,
    )
```

```python
import functools

import jax
import jax.numpy as jnp
from jax import lax
from jax.experimental import pallas as pl
from jax.experimental.pallas import tpu as pltpu
from jax.sharding import Mesh
from jax.sharding import PartitionSpec as P

EPS = 1e-06
X, Z, Y, CORE = 4, 8, 4, 2
DH, FF, HEADS = 320, 320, 16
LOCAL = FF // (X * Z)
BLOCK = FF // X
WIN = 384
LANES = 2 * DH
VMEM = 28 << 20
F32, BF16 = jnp.float32, jnp.bfloat16
NT = (((1,), (1,)), ((), ()))


def shifted(array, axis, by):
    n = lax.axis_size(axis)
    return lax.ppermute(array, axis, [(i, (i - by) % n) for i in range(n)])


def gathered_z(copies):
    every = lax.all_to_all(copies, "z", 0, 0, tiled=True)
    return jnp.moveaxis(every.reshape(Z, 3, LOCAL, LANES), 0, 1).reshape(3, BLOCK, LANES)


def in_turn(value, *first):
    return lax.optimization_barrier((value, *first))[0]


def own_lanes(head):
    lane = lax.broadcasted_iota(jnp.int32, (BLOCK, WIN), 1)
    return lane < DH if head == 0 else lane >= WIN - DH


def side_by_side(first, second):
    lane = lax.broadcasted_iota(jnp.int32, (first.shape[0], WIN - 256), 1)
    middle = jnp.where(lane < DH - 256, first[:, 256:], second[:, : WIN - 256])
    return jnp.concatenate([first[:, :256], middle, second[:, WIN - 256 :]], axis=1)


def update_body(blocks, tile, k_ref, v_ref, r_ref, *refs):
    w_refs, g_refs, (osq_ref, wgu, wd, agu, ad) = refs[:blocks], refs[blocks : 2 * blocks], refs[2 * blocks :]
    units = blocks * BLOCK
    sq = [jnp.zeros((1, LANES), F32) for _ in range(3)]
    for b, w_ref in enumerate(w_refs):
        for m in range(3):
            w = w_ref[m]
            wf = w.astype(F32)
            sq[m] += jnp.sum(wf * wf, axis=0, keepdims=True)
            for h in range(2):
                part = jnp.where(own_lanes(h), w[:, h * 256 : h * 256 + WIN], jnp.zeros((), BF16))
                if m < 2:
                    wgu[h, pl.ds(m * units + b * BLOCK, BLOCK), :] = part
                else:
                    wd[h, pl.ds(b * BLOCK, BLOCK), :] = part
    for m in range(3):
        osq_ref[m : m + 1, :] = sq[m]

    for at in range(0, k_ref.shape[0], tile):
        for h in range(2):
            k = k_ref[at : at + tile, h * 256 : h * 256 + WIN]
            v = v_ref[at : at + tile, h * 256 : h * 256 + WIN]
            rate = r_ref[h : h + 1, at : at + tile]
            gu = lax.dot_general(wgu[h], k, NT, preferred_element_type=F32)
            back = lax.dot_general(wd[h], v, NT, preferred_element_type=F32) * rate
            g, u = gu[:units], gu[units:]
            s = 0.5 * jnp.tanh(0.5 * g) + 0.5
            act = g * s
            slope = s + act * (1.0 - s)
            dgate = (back * u * slope).astype(BF16)
            dup = (back * act).astype(BF16)
            hidden = (act * u * rate).astype(BF16)
            ggu = jnp.dot(jnp.concatenate([dgate, dup], axis=0), k, preferred_element_type=F32)
            gd = jnp.dot(hidden, v, preferred_element_type=F32)
            agu[h] = ggu if at == 0 else agu[h] + ggu
            ad[h] = gd if at == 0 else ad[h] + gd

    for b, g_ref in enumerate(g_refs):
        for m in range(3):
            acc, at = (agu, m * units + b * BLOCK) if m < 2 else (ad, b * BLOCK)
            rows = pl.ds(at, BLOCK)
            g_ref[m] = side_by_side(acc[0, rows, :], acc[1, rows, :]).astype(BF16)


def update(keys, values, rates, blocks, tile=1024):
    tokens, n = keys.shape[0], len(blocks)
    vmem = pl.BlockSpec(memory_space=pltpu.VMEM)
    outs = pl.pallas_call(
        functools.partial(update_body, n, tile),
        in_specs=[vmem] * (3 + n),
        out_specs=[vmem] * (n + 1),
        out_shape=[jax.ShapeDtypeStruct((3, BLOCK, LANES), BF16)] * n + [jax.ShapeDtypeStruct((3, LANES), F32)],
        scratch_shapes=[
            pltpu.VMEM((2, 2 * n * BLOCK, WIN), BF16),
            pltpu.VMEM((2, n * BLOCK, WIN), BF16),
            pltpu.VMEM((2, 2 * n * BLOCK, WIN), F32),
            pltpu.VMEM((2, n * BLOCK, WIN), F32),
        ],
        cost_estimate=pl.CostEstimate(
            flops=48 * tokens * n * BLOCK * WIN, bytes_accessed=4 * tokens * LANES, transcendentals=2 * tokens * FF
        ),
        compiler_params=pltpu.CompilerParams(vmem_limit_bytes=VMEM),
        name="update",
    )(keys, values, rates, *blocks)
    return outs[:n], outs[n]


def apply_body(part, q_in, osq_ref, *refs):
    u_in, (o_ref, sq_ref, sc_ref, wgu, wd, q_ref, u_refs, q_sems, u_sems) = refs[:X], refs[X:]
    tokens = q_in.shape[0]
    fetches = [pltpu.make_async_copy(u, u_refs.at[b], u_sems.at[b]) for b, u in enumerate(u_in)]
    reads = [
        pltpu.make_async_copy(q_in.at[r : r + part, :], q_ref.at[r : r + part, :], q_sems.at[r // part])
        for r in range(0, tokens, part)
    ]
    for copy in fetches + reads:
        copy.start()
    wgu[:, FF:WIN, :] = jnp.zeros((2, WIN - FF, WIN), BF16)
    wgu[:, WIN + FF :, :] = jnp.zeros((2, WIN - FF, WIN), BF16)
    wd[:, FF:, :] = jnp.zeros((2, WIN - FF, WIN), BF16)
    for fetch in fetches:
        fetch.wait()
    for m in range(3):
        sq = jnp.zeros((1, LANES), F32)
        for b in range(X):
            wf = u_refs[b, m].astype(F32)
            sq += jnp.sum(wf * wf, axis=0, keepdims=True)
        sc = jnp.sqrt(osq_ref[m : m + 1, :]) * lax.rsqrt(sq + EPS)
        sc_ref[m : m + 1, :] = sc
        for b in range(X):
            for h in range(2):
                cols = slice(h * 256, h * 256 + WIN)
                if m < 2:
                    scaled = (u_refs[b, m, :, cols].astype(F32) * sc[:, cols]).astype(BF16)
                    scaled = jnp.where(own_lanes(h), scaled, jnp.zeros((), BF16))
                    wgu[h, pl.ds(m * WIN + b * BLOCK, BLOCK), :] = scaled
                else:
                    wd[h, pl.ds(b * BLOCK, BLOCK), :] = u_refs[b, m, :, cols]
    down = sc_ref[2:3, :]

    def project(rows, h):
        if h == 0:
            reads[rows.start // part].wait()
        q = q_ref[rows, h * 256 : h * 256 + WIN]
        return lax.dot_general(q, wgu[h], NT, preferred_element_type=F32)

    def finish(rows, outs):
        o = side_by_side(*outs) * down
        o_ref[rows, :] = o.astype(BF16)
        sq = o * o
        sq = sum(sq[:, c * 128 : (c + 1) * 128] for c in range(1, LANES // 128)) + sq[:, :128]
        for j in range(o.shape[0] // 128):
            at = rows.start // 128 + j
            sq_ref[at : at + 1, :] = jnp.sum(jnp.transpose(sq[j * 128 : (j + 1) * 128]), axis=0, keepdims=True)

    steps = [(slice(r, r + part), h) for r in range(0, tokens, part) for h in range(2)]
    ahead, outs = project(*steps[0]), []
    for i, (rows, h) in enumerate(steps):
        g, u = ahead[:, :WIN], ahead[:, WIN:]
        if i + 1 < len(steps):
            ahead = project(*steps[i + 1])
        mixed = (g * (0.5 * jnp.tanh(0.5 * g) + 0.5) * u).astype(BF16)
        outs.append(jnp.dot(mixed, wd[h], preferred_element_type=F32))
        if h == 1:
            finish(rows, outs)
            outs = []


def apply(queries, old_sq, blocks, part=512):
    tokens = queries.shape[0]
    vmem, hbm = pl.BlockSpec(memory_space=pltpu.VMEM), pl.BlockSpec(memory_space=pltpu.HBM)
    return pl.pallas_call(
        functools.partial(apply_body, part),
        in_specs=[hbm, vmem] + [hbm] * X,
        out_specs=[vmem] * 3,
        out_shape=[
            jax.ShapeDtypeStruct((tokens, LANES), BF16),
            jax.ShapeDtypeStruct((tokens // 128, 128), F32),
            jax.ShapeDtypeStruct((3, LANES), F32),
        ],
        scratch_shapes=[
            pltpu.VMEM((2, 2 * WIN, WIN), BF16),
            pltpu.VMEM((2, WIN, WIN), BF16),
            pltpu.VMEM((tokens, LANES), BF16),
            pltpu.VMEM((X, 3, BLOCK, LANES), BF16),
            pltpu.SemaphoreType.DMA((tokens // part,)),
            pltpu.SemaphoreType.DMA((X,)),
        ],
        cost_estimate=pl.CostEstimate(
            flops=12 * tokens * FF * WIN, bytes_accessed=6 * tokens * LANES, transcendentals=2 * tokens * FF
        ),
        compiler_params=pltpu.CompilerParams(vmem_limit_bytes=VMEM),
        name="apply",
    )(queries, old_sq, *blocks)


def scale_body(part, o_ref, gain_ref, *refs):
    sq_refs, (out_ref, out_vmem, sems) = refs[:X], refs[X:]
    spans = [slice(r, r + part) for r in range(0, o_ref.shape[0], part)]
    gain = gain_ref[...]
    sq = sum(r[...] for r in sq_refs[1:]) + sq_refs[0][...]
    scale = lax.rsqrt(sq / (HEADS * DH) + EPS)
    writes = []
    for i, span in enumerate(spans):
        for at in range(span.start, span.stop, 128):
            rows = slice(at, at + 128)
            across = jnp.transpose(jnp.broadcast_to(scale[at // 128 : at // 128 + 1], (128, 128)))
            for c in range(LANES // 128):
                cols = slice(c * 128, (c + 1) * 128)
                out_vmem[rows, cols] = (o_ref[rows, cols].astype(F32) * across * gain[:, cols]).astype(BF16)
        write = pltpu.make_async_copy(out_vmem.at[span, :], out_ref.at[span, :], sems.at[i])
        write.start()
        writes.append(write)
    for write in writes:
        write.wait()


def scaled_output(o, squares, gain, part=256):
    tokens = o.shape[0]
    vmem, hbm = pl.BlockSpec(memory_space=pltpu.VMEM), pl.BlockSpec(memory_space=pltpu.HBM)
    return pl.pallas_call(
        functools.partial(scale_body, part),
        in_specs=[vmem] * (2 + len(squares)),
        out_specs=hbm,
        out_shape=jax.ShapeDtypeStruct((tokens, LANES), BF16),
        scratch_shapes=[
            pltpu.VMEM((tokens, LANES), BF16),
            pltpu.SemaphoreType.DMA((tokens // part,)),
        ],
        compiler_params=pltpu.CompilerParams(vmem_limit_bytes=VMEM),
        name="scale",
    )(o, gain, *squares)


def pack_body(gate_ref, up_ref, down_ref, own_ref, copies_ref):
    rows = []
    for w_ref in (gate_ref, up_ref, down_ref):
        w = w_ref[...].astype(F32)
        rows.append(jnp.concatenate([w[:, 0, :], w[:, 1, :]], axis=1))
    own = jnp.concatenate(rows, axis=0).astype(BF16)
    own_ref[...] = own
    for z in range(Z):
        copies_ref[z] = own


def packed(weights):
    return pl.pallas_call(
        pack_body,
        out_shape=[
            jax.ShapeDtypeStruct((3 * LOCAL, LANES), BF16),
            jax.ShapeDtypeStruct((Z, 3 * LOCAL, LANES), BF16),
        ],
        name="pack",
    )(*weights)


def per_device(keys, values, queries, rates, w_gate, w_up, w_down, gain):
    own, copies = packed((w_gate, w_up, w_down))
    rates = rates.T
    here = gathered_z(copies)
    across = shifted(here, "x", 2)
    sides = shifted(here, "x", 1), shifted(here, "x", 3)
    (g0,), sq_a = update(keys, values, rates, (here,))
    (g2,), sq_b = update(keys, values, in_turn(rates, g0), (across,))
    r2 = shifted(g2, "x", 2)
    (g1, g3), sq_c = update(keys, values, in_turn(rates, g2), sides)
    r1, r3 = shifted(g1, "x", 3), shifted(g3, "x", 1)
    total = lax.optimization_barrier(g0.astype(F32) + r2.astype(F32)) + r1.astype(F32) + r3.astype(F32)
    old_sq = sq_a + sq_b + sq_c
    pieces = jnp.moveaxis(total.astype(BF16).reshape(3, Z, LOCAL, LANES), 1, 0).reshape(Z, 3 * LOCAL, LANES)
    pieces = lax.all_to_all(pieces, "z", 0, 0, tiled=True)
    updated = own.astype(F32) + jnp.sum(pieces.astype(F32), axis=0)

    here = gathered_z(jnp.broadcast_to(updated.astype(BF16)[None], (Z, 3 * LOCAL, LANES)))
    new = [here] + [shifted(here, "x", s) for s in (1, 3, 2)]
    queries = pltpu.with_memory_space_constraint(queries, pltpu.HBM)
    new[1] = pltpu.with_memory_space_constraint(new[1], pltpu.HBM)
    new[3] = pltpu.with_memory_space_constraint(new[3], pltpu.HBM)
    o, squares, scale = apply(queries, old_sq, new)
    squares = squares.reshape(-1)
    squares += shifted(squares, "core", 1)
    squares = [squares] + [shifted(squares, "y", s) for s in (2, 1, 3)]
    output = scaled_output(o, [s.reshape(-1, 128) for s in squares], gain.reshape(1, LANES))
    fresh = (updated.reshape(3, LOCAL, LANES) * scale[:, None, :]).astype(BF16).reshape(3, LOCAL, 2, DH)
    return output, fresh[0], fresh[1], fresh[2]


def solution(mesh):
    split = Mesh(mesh.devices.reshape(X, Z, Y, CORE), ("x", "z", "y", "core"))
    ctx, head = ("x", "z"), ("y", "core")
    weight = P(ctx, head, None)
    return jax.shard_map(
        per_device,
        mesh=split,
        in_specs=(P(ctx, head),) * 4 + (weight,) * 3 + (P(head),),
        out_specs=(P(ctx, head),) + (weight,) * 3,
        check_vma=False,
    )
```
